32 devices in a mesh: grp: 2 (over x), seq: 16 (over z, y, core).
Axes of the slice: x: 2, y: 2, z: 4, core: 2. Of those that a mesh axis runs over, the one named last changes fastest.
Arguments:
- tokens: bfloat16 [16384, 1024], P(('grp', 'seq')), parts along dimension 0, may hold values from -6 to 6
- value_weight: bfloat16 [1024, 1024], replicated, may hold values from -0.1875 to 0.1875
- gate_weight: bfloat16 [1024, 1024], replicated, may hold values from -0.1875 to 0.1875
- out_weight: bfloat16 [1024, 1024], replicated, may hold values from -0.1875 to 0.1875
- kernel_weight: bfloat16 [1024, 16], replicated, may hold values from -0.1875 to 0.1875
- kernel_bias: float32 [16], replicated, may hold values from -4 to 4
Outputs:
- mixed: bfloat16 [16384, 1024], P(('grp', 'seq')), parts along dimension 0
The draws below stay inside these ranges and needn't reach their ends.
There are 2 independent parts, one for each index of `grp`. The reference program is written for one: setup_inputs(seed, part) draws one part's arguments, and reference() takes and returns one part's arrays. A program takes and returns all parts, laid end to end along the dimension named above; an argument that names none is the same for every part. Nothing has to cross between parts.
All inputs are finite; a program needn't handle non-finite values.
Results may differ from the reference program's by a relative error of at most 0.0071.
Values may be sent and summed in bfloat16 or wider, within the bound.
A program may use at most 128 MiB of HBM per device.

```python
import jax
import jax.numpy as jnp

D = 1024
HEADS = 16
HS = 64
TOKENS = 8192


def block_levels(rng, extent, split, low, top_value):
    def one(position, blocks):
        steps = jax.random.uniform(jax.random.fold_in(jax.random.fold_in(rng, 6), position), (blocks,), jnp.float32, low / len(split), top_value / len(split))
        return jnp.repeat(jnp.exp(steps), extent[position] // blocks).reshape((-1,) + (1,) * (len(extent) - position - 1))

    factor_of = one(*split[0])
    for cut in split[1:]:
        factor_of = factor_of * one(*cut)
    return factor_of


def scatter_about(rng, dims, width, reach, split=(), dtype=jnp.bfloat16):
    level = block_levels(rng, dims, split, -0.22, 0.18) if split else 1.0
    array = jax.random.normal(rng, dims, jnp.float32) * width * level
    return jnp.minimum(jnp.maximum(array, -reach), reach).astype(dtype)


def setup_inputs(seed: int = 0, part: int = 0) -> dict:
    arg_keys = jax.random.split(jax.random.key(seed), 7)
    own_keys = jax.random.split(jax.random.fold_in(arg_keys[6], part), 7)
    tokens = scatter_about(own_keys[0], (TOKENS, D), 1.0, 6.0, ((0, 16),))
    value_weight = scatter_about(arg_keys[1], (D, D), D ** -0.5, 0.1875)
    gate_weight = scatter_about(arg_keys[2], (D, D), D ** -0.5, 0.1875)
    out_weight = scatter_about(arg_keys[3], (D, D), D ** -0.5, 0.1875)
    kernel_weight = scatter_about(arg_keys[4], (D, HEADS), D ** -0.5, 0.1875)
    kernel_bias = scatter_about(arg_keys[5], (HEADS,), 1.0, 4.0, (), jnp.float32)
    return dict(tokens=tokens, value_weight=value_weight, gate_weight=gate_weight, out_weight=out_weight, kernel_weight=kernel_weight, kernel_bias=kernel_bias)


def reference(tokens, value_weight, gate_weight, out_weight, kernel_weight, kernel_bias):
    values = jnp.dot(tokens, value_weight, preferred_element_type=jnp.float32).astype(jnp.bfloat16)
    gate = jnp.dot(tokens, gate_weight, preferred_element_type=jnp.float32)
    logits = jnp.dot(tokens, kernel_weight, preferred_element_type=jnp.float32) + kernel_bias
    kernel = (jnp.tanh(logits) * (TOKENS ** -0.5)).astype(jnp.bfloat16)
    kernel_freq = jnp.fft.rfft(kernel.astype(jnp.float32), axis=0)
    value_freq = jnp.fft.rfft(values.astype(jnp.float32), axis=0)
    product = value_freq.reshape(-1, HEADS, HS) * kernel_freq[:, :, None]
    conv = jnp.fft.irfft(product, n=TOKENS, axis=0).reshape(TOKENS, D).astype(jnp.bfloat16)
    gated = (conv.astype(jnp.float32) * jax.nn.silu(gate)).astype(jnp.bfloat16)
    return jnp.dot(gated, out_weight, preferred_element_type=jnp.float32).astype(jnp.bfloat16)
```

```python
import functools

import jax
import jax.numpy as jnp
from jax import lax
from jax.experimental import pallas as pl
from jax.experimental.pallas import tpu as pltpu
from jax.sharding import PartitionSpec as P

MESH = pl.DeviceIdType.MESH


def convolve_kernel(n, values_ref, lag_ref, out_ref, held, lags, band, result, sems):
    width, rows = values_ref.shape[1:]
    length = n * rows
    me = lax.axis_index("seq")
    barrier = pltpu.get_barrier_semaphore()

    def greet(step, carry):
        pl.semaphore_signal(barrier, inc=1, device_id={"seq": lax.rem(me + step, n)}, device_id_type=MESH)
        return carry

    lax.fori_loop(1, n, greet, 0)
    pl.semaphore_wait(barrier, n - 1)

    def copy(kind, source, target, step, peer):
        return pltpu.make_async_remote_copy(
            src_ref=source,
            dst_ref=target,
            send_sem=sems.at[2 * kind, step],
            recv_sem=sems.at[2 * kind + 1, step],
            device_id={"seq": peer},
            device_id_type=MESH,
        )

    def lag_copy(step):
        peer = lax.rem(me + step, n)
        return copy(0, lag_ref.at[peer], lags.at[me], step, peer)

    def value_copy(step):
        peer = lax.rem(me + step, n)
        return copy(1, values_ref.at[peer], held.at[me], step, peer)

    def back_copy(step):
        peer = lax.rem(me + step, n)
        return copy(2, result.at[peer], out_ref.at[me], step, peer)

    def loop(action):
        def run(step, carry):
            action(step)
            return carry

        lax.fori_loop(1, n, run, 0)

    loop(lambda step: lag_copy(step).start())
    loop(lambda step: value_copy(step).start())
    lags[me] = lag_ref[me]
    held[me] = values_ref[me]
    loop(lambda step: lag_copy(step).wait())
    half = 128
    row = jnp.concatenate([lags[place] for place in range(n)], axis=1)
    row = jnp.concatenate([row[:, length - rows - half :], row], axis=1)
    tile = 512
    for start in range(0, length + rows, tile):
        size = min(tile, length + rows - start)
        piece = jnp.broadcast_to(row[:, start : start + size + half], (half, size + half))
        turned = pltpu.roll(piece, 0, 1, stride=1, stride_axis=0)[:, half:].astype(jnp.bfloat16)
        band[:, start : start + size] = turned
    loop(lambda step: value_copy(step).wait())
    held[n : 2 * n] = held[0:n]

    group = max(1, 256 // width)
    reach = min(n, 16)

    def outputs(index, carry):
        first = index * group
        total = None
        for base in range(0, n, reach):
            left = jnp.concatenate(
                [held[pl.ds(first + place, group)].reshape(group * width, rows) for place in range(base, base + reach)],
                axis=1,
            )
            right = jnp.concatenate(
                [
                    band[:, pl.ds((rows - at) if at <= rows else length + rows - at, rows)]
                    for at in range(base * rows, (base + reach) * rows, half)
                ],
                axis=0,
            )
            term = jnp.dot(left, right, preferred_element_type=jnp.float32)
            total = term if total is None else total + term
        result[pl.ds(first, group)] = total.astype(jnp.bfloat16).reshape(group, width, rows)
        return carry

    lax.fori_loop(0, n // group, outputs, 0)
    loop(lambda step: back_copy(step).start())
    out_ref[me] = result[me]
    loop(lambda step: back_copy(step).wait())


def body(tokens, value_weight, gate_weight, out_weight, kernel_weight, kernel_bias):
    rows, model_width = tokens.shape
    heads = kernel_weight.shape[1]
    n = lax.axis_size("seq")
    width = model_width // n
    length = rows * n
    contract = (((0,), (1,)), ((), ()))
    values_t = lax.dot_general(
        value_weight, tokens, contract, preferred_element_type=jnp.float32
    ).astype(jnp.bfloat16)
    gate_t = lax.dot_general(gate_weight, tokens, contract, preferred_element_type=jnp.float32)
    logits = (
        lax.dot_general(kernel_weight, tokens, contract, preferred_element_type=jnp.float32)
        + kernel_bias[:, None]
    )
    lags = (jnp.tanh(logits) * length ** (-0.5)).astype(jnp.bfloat16).astype(jnp.float32)
    lags = jnp.repeat(lags, n // heads, axis=0).reshape(n, 1, rows)
    vmem = pl.BlockSpec(memory_space=pltpu.VMEM)
    conv_t = pl.pallas_call(
        functools.partial(convolve_kernel, n),
        out_shape=jax.ShapeDtypeStruct((n, width, rows), jnp.bfloat16),
        in_specs=[vmem, vmem],
        out_specs=vmem,
        scratch_shapes=[
            pltpu.VMEM((2 * n, width, rows), jnp.bfloat16),
            pltpu.VMEM((n, 1, rows), jnp.float32),
            pltpu.VMEM((128, length + rows), jnp.bfloat16),
            pltpu.VMEM((n, width, rows), jnp.bfloat16),
            pltpu.SemaphoreType.DMA((6, n)),
        ],
        compiler_params=pltpu.CompilerParams(
            collective_id=0, has_side_effects=True, vmem_limit_bytes=60 * 2**20
        ),
    )(values_t.reshape(n, width, rows), lags)
    conv_t = conv_t.reshape(model_width, rows)
    gated_t = (conv_t.astype(jnp.float32) * jax.nn.silu(gate_t)).astype(jnp.bfloat16)
    mixed = lax.dot_general(
        gated_t, out_weight, (((0,), (0,)), ((), ())), preferred_element_type=jnp.float32
    )
    return mixed.astype(jnp.bfloat16)


def solution(mesh):
    placed = (P(("grp", "seq"), None), P(), P(), P(), P(), P())
    return jax.shard_map(
        body, mesh=mesh, in_specs=placed, out_specs=P(("grp", "seq"), None), check_vma=False
    )
```

```python
import functools

import jax
import jax.numpy as jnp
from jax import lax
from jax.experimental import pallas as pl
from jax.experimental.pallas import tpu as pltpu
from jax.sharding import PartitionSpec as P

MESH = pl.DeviceIdType.MESH
LANES = 128
BLOCK = 256
CHUNKS = 4


def layer_kernel(
    n,
    heads,
    tokens_hbm,
    value_hbm,
    gate_hbm,
    out_hbm,
    head_ref,
    bias_ref,
    mixed_ref,
    tokens,
    value_w,
    gate_w,
    out_w,
    outgoing,
    held,
    lag_send,
    lags,
    band,
    open_gate,
    result,
    returned,
    total,
    load_sems,
    lag_sems,
    sems,
):
    rows, model = tokens.shape
    chunks, _, wide, _ = outgoing.shape
    width = chunks * wide
    length = n * rows
    per = BLOCK // width
    blocks = n // per
    share = n // heads
    me = lax.axis_index("seq")
    mine = me // per
    order = sorted(range(blocks), key=lambda off: (-min(off, blocks - off), off))

    def place(off):
        return lax.rem(mine + off, blocks)

    def load(source, target, slot):
        return pltpu.make_async_copy(source, target, load_sems.at[slot])

    def value_load(off):
        columns = pl.ds(pl.multiple_of(place(off) * BLOCK, BLOCK), BLOCK)
        return load(value_hbm.at[:, columns], value_w.at[off], 3 + off)

    tokens_load = load(tokens_hbm, tokens, 0)
    gate_load = load(gate_hbm, gate_w, 1)
    out_load = load(out_hbm, out_w, 2)
    tokens_load.start()
    for off in order:
        value_load(off).start()
    gate_load.start()
    out_load.start()

    barrier = pltpu.get_barrier_semaphore()

    def loop(action):
        def run(step, carry):
            action(step)
            return carry

        lax.fori_loop(1, n, run, 0)

    loop(
        lambda step: pl.semaphore_signal(
            barrier, inc=1, device_id={"seq": lax.rem(me + step, n)}, device_id_type=MESH
        )
    )

    def lag_copy(step):
        peer = lax.rem(me + step, n)
        return pltpu.make_async_remote_copy(
            src_ref=lag_send.at[peer // share],
            dst_ref=lags.at[me],
            send_sem=lag_sems.at[0, step],
            recv_sem=lag_sems.at[1, step],
            device_id={"seq": peer},
            device_id_type=MESH,
        )

    def remote(kind, source, target, chunk, step):
        peer = lax.rem(me + step, n)
        return pltpu.make_async_remote_copy(
            src_ref=source.at[chunk, peer],
            dst_ref=target.at[chunk, me],
            send_sem=sems.at[2 * kind, chunk, step],
            recv_sem=sems.at[2 * kind + 1, chunk, step],
            device_id={"seq": peer},
            device_id_type=MESH,
        )

    def value_copy(chunk, step):
        return remote(0, outgoing, held, chunk, step)

    def back_copy(chunk, step):
        return remote(1, result, returned, chunk, step)

    def send_block(off, chunk, make):
        inside = lax.rem(me, per)
        for turn in range(1 if off == 0 else 0, per):
            peer = place(off) * per + lax.rem(inside + turn, per)
            make(chunk, lax.rem(peer - me + n, n)).start()

    tokens_load.wait()
    logits = jnp.dot(tokens[...], head_ref[...], preferred_element_type=jnp.float32) + bias_ref[...]
    made = (jnp.tanh(logits) * length ** (-0.5)).astype(jnp.bfloat16).astype(jnp.float32).T
    for head in range(heads):
        lag_send[head] = made[head : head + 1]
    pl.semaphore_wait(barrier, n - 1)
    loop(lambda step: lag_copy(step).start())
    lags[me] = lag_send[me // share]

    for off in order:
        value_load(off).wait()
        block = jnp.dot(tokens[...], value_w[off], preferred_element_type=jnp.float32)
        block = block.astype(jnp.bfloat16).T.reshape(per, chunks, wide, rows)
        for chunk in range(chunks):
            outgoing[chunk, pl.ds(place(off) * per, per)] = block[:, chunk]
        send_block(off, 0, value_copy)
    for chunk in range(1, chunks):
        for off in order:
            send_block(off, chunk, value_copy)
    for chunk in range(chunks):
        held[chunk, me] = outgoing[chunk, me]

    loop(lambda step: lag_copy(step).wait())
    row = jnp.concatenate([lags[source] for source in range(n)], axis=1)
    row = jnp.concatenate([row[:, length - rows - LANES :], row], axis=1)
    for start in range(0, length + rows, rows):
        piece = jnp.broadcast_to(row[:, start : start + rows + LANES], (LANES, rows + LANES))
        turned = pltpu.roll(piece, 0, 1, stride=1, stride_axis=0)[:, LANES:]
        band[:, start : start + rows] = turned.astype(jnp.bfloat16)

    gate_load.wait()
    for part in range(model // BLOCK):
        gate = jnp.dot(
            tokens[...], gate_w[:, part * BLOCK : (part + 1) * BLOCK], preferred_element_type=jnp.float32
        )
        gate = (gate / (1.0 + jnp.exp(-gate))).T.reshape(per, chunks, wide, rows)
        for chunk in range(chunks):
            open_gate[chunk, part * per : (part + 1) * per] = gate[:, chunk]

    group = min(n, max(1, BLOCK // wide))
    reach = min(n, 16)

    def convolve(chunk, carry):
        loop(lambda step: value_copy(chunk, step).wait())
        held[chunk, n : 2 * n] = held[chunk, 0:n]

        def outputs(index, inner):
            first = index * group
            summed = None
            for base in range(0, n, reach):
                left = jnp.concatenate(
                    [
                        held[chunk, pl.ds(first + at, group)].reshape(group * wide, rows)
                        for at in range(base, base + reach)
                    ],
                    axis=1,
                )
                right = jnp.concatenate(
                    [
                        band[:, pl.ds((rows - at) if at <= rows else length + rows - at, rows)]
                        for at in range(base * rows, (base + reach) * rows, LANES)
                    ],
                    axis=0,
                )
                term = jnp.dot(left, right, preferred_element_type=jnp.float32)
                summed = term if summed is None else summed + term
            result[chunk, pl.ds(first, group)] = summed.astype(jnp.bfloat16).reshape(group, wide, rows)
            return inner

        lax.fori_loop(0, n // group, outputs, 0)
        for off in order:
            send_block(off, chunk, back_copy)
        returned[chunk, me] = result[chunk, me]
        return carry

    lax.fori_loop(0, chunks, convolve, 0)

    out_load.wait()
    for chunk in range(chunks):
        loop(lambda step: back_copy(chunk, step).wait())
        gated = (returned[chunk].astype(jnp.float32) * open_gate[chunk]).astype(jnp.bfloat16)
        weight = out_w[:, chunk].reshape(n * wide, model)
        term = jnp.dot(gated.reshape(n * wide, rows).T, weight, preferred_element_type=jnp.float32)
        if chunk > 0:
            term = total[...] + term
        if chunk < chunks - 1:
            total[...] = term
        else:
            mixed_ref[...] = term.astype(jnp.bfloat16)


def body(tokens, value_weight, gate_weight, out_weight, kernel_weight, kernel_bias):
    rows, model = tokens.shape
    heads = kernel_weight.shape[1]
    n = lax.axis_size("seq")
    width = model // n
    chunks = max(1, min(CHUNKS, width // 16))
    wide = width // chunks
    length = rows * n
    per = BLOCK // width
    vmem = pl.BlockSpec(memory_space=pltpu.VMEM)
    anywhere = pl.BlockSpec(memory_space=pl.ANY)
    half = jnp.bfloat16
    return pl.pallas_call(
        functools.partial(layer_kernel, n, heads),
        out_shape=jax.ShapeDtypeStruct((rows, model), half),
        in_specs=[anywhere] * 4 + [vmem] * 2,
        out_specs=vmem,
        scratch_shapes=[
            pltpu.VMEM((rows, model), half),
            pltpu.VMEM((n // per, model, BLOCK), half),
            pltpu.VMEM((model, model), half),
            pltpu.VMEM((n, chunks, wide, model), half),
            pltpu.VMEM((chunks, n, wide, rows), half),
            pltpu.VMEM((chunks, 2 * n, wide, rows), half),
            pltpu.VMEM((heads, 1, rows), jnp.float32),
            pltpu.VMEM((n, 1, rows), jnp.float32),
            pltpu.VMEM((LANES, length + rows), half),
            pltpu.VMEM((chunks, n, wide, rows), jnp.float32),
            pltpu.VMEM((chunks, n, wide, rows), half),
            pltpu.VMEM((chunks, n, wide, rows), half),
            pltpu.VMEM((rows, model), jnp.float32),
            pltpu.SemaphoreType.DMA((3 + n // per,)),
            pltpu.SemaphoreType.DMA((2, n)),
            pltpu.SemaphoreType.DMA((4, chunks, n)),
        ],
        compiler_params=pltpu.CompilerParams(
            collective_id=0, has_side_effects=True, vmem_limit_bytes=60 * 2**20
        ),
    )(
        tokens,
        value_weight,
        gate_weight,
        out_weight.reshape(n, chunks, wide, model),
        kernel_weight,
        kernel_bias.reshape(1, heads),
    )


def solution(mesh):
    placed = (P(("grp", "seq"), None), P(), P(), P(), P(), P())
    return jax.shard_map(
        body, mesh=mesh, in_specs=placed, out_specs=P(("grp", "seq"), None), check_vma=False
    )
```

```python
import functools

import jax
import jax.numpy as jnp
from jax import lax
from jax.experimental import pallas as pl
from jax.experimental.pallas import tpu as pltpu
from jax.sharding import PartitionSpec as P

MESH = pl.DeviceIdType.MESH
LANES = 128
BLOCK = 256
CHUNKS = 2


def layer_kernel(
    n,
    heads,
    tokens_hbm,
    value_hbm,
    gate_hbm,
    out_hbm,
    head_ref,
    bias_ref,
    mixed_ref,
    tokens,
    value_w,
    gate_w,
    out_w,
    outgoing,
    held,
    lag_send,
    lags,
    band,
    open_gate,
    result,
    returned,
    total,
    load_sems,
    lag_sems,
    sems,
):
    rows, model = tokens.shape
    chunks, _, wide, _ = outgoing.shape
    width = chunks * wide
    length = n * rows
    per = BLOCK // width
    blocks = n // per
    share = n // heads
    me = lax.axis_index("seq")
    mine = me // per
    side = blocks // 2
    order = range(blocks)

    def place(off):
        near = mine // side
        if off < side:
            return (1 - near) * side + lax.rem(mine + off, side)
        return near * side + lax.rem(mine + off + 1, side)

    def load(source, target, slot):
        return pltpu.make_async_copy(source, target, load_sems.at[slot])

    def value_load(off):
        columns = pl.ds(pl.multiple_of(place(off) * BLOCK, BLOCK), BLOCK)
        return load(value_hbm.at[:, columns], value_w.at[off], 3 + off)

    tokens_load = load(tokens_hbm, tokens, 0)
    gate_load = load(gate_hbm, gate_w, 1)
    out_load = load(out_hbm, out_w, 2)
    barrier = pltpu.get_barrier_semaphore()

    def loop(action):
        def run(step, carry):
            action(step)
            return carry

        lax.fori_loop(1, n, run, 0)

    loop(
        lambda step: pl.semaphore_signal(
            barrier, inc=1, device_id={"seq": lax.rem(me + step, n)}, device_id_type=MESH
        )
    )

    tokens_load.start()
    for off in order:
        value_load(off).start()

    def lag_copy(step):
        peer = lax.rem(me + step, n)
        return pltpu.make_async_remote_copy(
            src_ref=lag_send.at[peer // share],
            dst_ref=lags.at[me],
            send_sem=lag_sems.at[0, step],
            recv_sem=lag_sems.at[1, step],
            device_id={"seq": peer},
            device_id_type=MESH,
        )

    def remote(kind, source, target, chunk, step):
        peer = lax.rem(me + step, n)
        return pltpu.make_async_remote_copy(
            src_ref=source.at[chunk, peer],
            dst_ref=target.at[chunk, me],
            send_sem=sems.at[2 * kind, chunk, step],
            recv_sem=sems.at[2 * kind + 1, chunk, step],
            device_id={"seq": peer},
            device_id_type=MESH,
        )

    def value_copy(chunk, step):
        return remote(0, outgoing, held, chunk, step)

    def back_copy(chunk, step):
        return remote(1, result, returned, chunk, step)

    def send_block(off, chunk, make):
        inside = lax.rem(me, per)
        for turn in range(1 if off == blocks - 1 else 0, per):
            peer = place(off) * per + lax.rem(inside + turn, per)
            make(chunk, lax.rem(peer - me + n, n)).start()

    tokens_load.wait()
    for off in order:
        value_load(off).wait()
        block = jnp.dot(tokens[...], value_w[off], preferred_element_type=jnp.float32)
        block = block.astype(jnp.bfloat16).T.reshape(per, chunks, wide, rows)
        for chunk in range(chunks):
            outgoing[chunk, pl.ds(place(off) * per, per)] = block[:, chunk]
        if off == 0:
            pl.semaphore_wait(barrier, n - 1)
        send_block(off, 0, value_copy)
        if off == 0:
            gate_load.start()
            out_load.start()
            logits = lax.dot_general(
                head_ref[...], tokens[...], (((1,), (1,)), ((), ())), preferred_element_type=jnp.float32
            )
            for head in range(heads):
                made = jnp.tanh(logits[head : head + 1] + bias_ref[0, head]) * length ** (-0.5)
                lag_send[head] = made.astype(jnp.bfloat16).astype(jnp.float32)
            loop(lambda step: lag_copy(step).start())
            lags[me] = lag_send[me // share]
    for chunk in range(1, chunks):
        for off in order:
            send_block(off, chunk, value_copy)
    for chunk in range(chunks):
        held[chunk, me] = outgoing[chunk, me]

    loop(lambda step: lag_copy(step).wait())
    row = jnp.concatenate([lags[source] for source in range(n)], axis=1)
    row = jnp.concatenate([row[:, length - rows - LANES :], row], axis=1)
    for start in range(0, length + rows, rows):
        piece = jnp.broadcast_to(row[:, start : start + rows + LANES], (LANES, rows + LANES))
        turned = pltpu.roll(piece, 0, 1, stride=1, stride_axis=0)[:, LANES:]
        band[:, start : start + rows] = turned.astype(jnp.bfloat16)

    gate_load.wait()
    for part in range(model // BLOCK):
        gate = jnp.dot(
            tokens[...], gate_w[:, part * BLOCK : (part + 1) * BLOCK], preferred_element_type=jnp.float32
        )
        gate = (gate / (1.0 + jnp.exp(-gate))).T.reshape(per, chunks, wide, rows)
        for chunk in range(chunks):
            open_gate[chunk, part * per : (part + 1) * per] = gate[:, chunk]

    group = min(n, max(1, BLOCK // wide))
    reach = min(n, 16)

    def convolve(chunk, carry):
        loop(lambda step: value_copy(chunk, step).wait())
        held[chunk, n : 2 * n] = held[chunk, 0:n]

        def outputs(index, inner):
            first = index * group
            summed = None
            for base in range(0, n, reach):
                left = jnp.concatenate(
                    [
                        held[chunk, pl.ds(first + at, group)].reshape(group * wide, rows)
                        for at in range(base, base + reach)
                    ],
                    axis=1,
                )
                right = jnp.concatenate(
                    [
                        band[:, pl.ds((rows - at) if at <= rows else length + rows - at, rows)]
                        for at in range(base * rows, (base + reach) * rows, LANES)
                    ],
                    axis=0,
                )
                term = jnp.dot(left, right, preferred_element_type=jnp.float32)
                summed = term if summed is None else summed + term
            result[chunk, pl.ds(first, group)] = summed.astype(jnp.bfloat16).reshape(group, wide, rows)
            return inner

        lax.fori_loop(0, n // group, outputs, 0)
        for off in order:
            send_block(off, chunk, back_copy)
        returned[chunk, me] = result[chunk, me]
        return carry

    lax.fori_loop(0, chunks, convolve, 0)

    out_load.wait()
    part = n // 2
    for chunk in range(chunks):
        for far in range(2):
            base = (me // part) * part if far == 0 else (1 - me // part) * part

            def arrive(index, carry):
                step = lax.rem(me - (base + index) + n, n)

                @pl.when(step > 0)
                def _():
                    back_copy(chunk, step).wait_recv()

                return carry

            lax.fori_loop(0, part, arrive, 0)
            chosen = pl.ds(base, part)
            gated = returned[chunk, chosen].astype(jnp.float32) * open_gate[chunk, chosen]
            gated = gated.astype(jnp.bfloat16).reshape(part * wide, rows).T
            weight = out_w[chosen, chunk].reshape(part * wide, model)
            term = jnp.dot(gated, weight, preferred_element_type=jnp.float32)
            if chunk + far > 0:
                term = total[...] + term
            if chunk + far < chunks:
                total[...] = term
            else:
                mixed_ref[...] = term.astype(jnp.bfloat16)
    for chunk in range(chunks):
        loop(lambda step: back_copy(chunk, step).wait_send())


def body(tokens, value_weight, gate_weight, out_weight, kernel_weight, kernel_bias):
    rows, model = tokens.shape
    heads = kernel_weight.shape[1]
    n = lax.axis_size("seq")
    width = model // n
    chunks = max(1, min(CHUNKS, width // 16))
    wide = width // chunks
    length = rows * n
    per = BLOCK // width
    vmem = pl.BlockSpec(memory_space=pltpu.VMEM)
    anywhere = pl.BlockSpec(memory_space=pl.ANY)
    half = jnp.bfloat16
    return pl.pallas_call(
        functools.partial(layer_kernel, n, heads),
        out_shape=jax.ShapeDtypeStruct((rows, model), half),
        in_specs=[anywhere] * 4 + [vmem, pl.BlockSpec(memory_space=pltpu.SMEM)],
        out_specs=vmem,
        scratch_shapes=[
            pltpu.VMEM((rows, model), half),
            pltpu.VMEM((n // per, model, BLOCK), half),
            pltpu.VMEM((model, model), half),
            pltpu.VMEM((n, chunks, wide, model), half),
            pltpu.VMEM((chunks, n, wide, rows), half),
            pltpu.VMEM((chunks, 2 * n, wide, rows), half),
            pltpu.VMEM((heads, 1, rows), jnp.float32),
            pltpu.VMEM((n, 1, rows), jnp.float32),
            pltpu.VMEM((LANES, length + rows), half),
            pltpu.VMEM((chunks, n, wide, rows), jnp.float32),
            pltpu.VMEM((chunks, n, wide, rows), half),
            pltpu.VMEM((chunks, n, wide, rows), half),
            pltpu.VMEM((rows, model), jnp.float32),
            pltpu.SemaphoreType.DMA((3 + n // per,)),
            pltpu.SemaphoreType.DMA((2, n)),
            pltpu.SemaphoreType.DMA((4, chunks, n)),
        ],
        compiler_params=pltpu.CompilerParams(
            collective_id=0, has_side_effects=True, vmem_limit_bytes=60 * 2**20
        ),
    )(
        tokens,
        value_weight,
        gate_weight,
        out_weight.reshape(n, chunks, wide, model),
        kernel_weight.T,
        kernel_bias.reshape(1, heads),
    )


def solution(mesh):
    placed = (P(("grp", "seq"), None), P(), P(), P(), P(), P())
    return jax.shard_map(
        body, mesh=mesh, in_specs=placed, out_specs=P(("grp", "seq"), None), check_vma=False
    )
```

```python
import functools

import jax
import jax.numpy as jnp
from jax import lax
from jax.experimental import pallas as pl
from jax.experimental.pallas import tpu as pltpu
from jax.sharding import PartitionSpec as P

MESH = pl.DeviceIdType.MESH
LANES = 128
BLOCK = 256
CHUNKS = 2


def layer_kernel(
    n,
    heads,
    tokens_hbm,
    value_hbm,
    gate_hbm,
    out_hbm,
    head_ref,
    bias_ref,
    mixed_ref,
    tokens,
    value_w,
    gate_w,
    out_w,
    outgoing,
    held,
    lag_send,
    lags,
    band,
    open_gate,
    result,
    returned,
    total,
    load_sems,
    lag_sems,
    sems,
):
    rows, model = tokens.shape
    chunks, _, wide, _ = outgoing.shape
    width = chunks * wide
    length = n * rows
    per = BLOCK // width
    blocks = n // per
    share = n // heads
    me = lax.axis_index("seq")
    mine = me // per
    distance = sorted(range(blocks), key=lambda off: (-min(off, blocks - off), off))
    order = range(blocks)

    def place(off):
        return lax.rem(mine + distance[off], blocks)

    def load(source, target, slot):
        return pltpu.make_async_copy(source, target, load_sems.at[slot])

    def value_load(off):
        columns = pl.ds(pl.multiple_of(place(off) * BLOCK, BLOCK), BLOCK)
        return load(value_hbm.at[:, columns], value_w.at[off], 3 + off)

    tokens_load = load(tokens_hbm, tokens, 0)
    gate_load = load(gate_hbm, gate_w, 1)
    out_load = load(out_hbm, out_w, 2)
    barrier = pltpu.get_barrier_semaphore()

    def loop(action):
        def run(step, carry):
            action(step)
            return carry

        lax.fori_loop(1, n, run, 0)

    loop(
        lambda step: pl.semaphore_signal(
            barrier, inc=1, device_id={"seq": lax.rem(me + step, n)}, device_id_type=MESH
        )
    )

    tokens_load.start()
    for off in order:
        value_load(off).start()

    def lag_copy(step):
        peer = lax.rem(me + step, n)
        return pltpu.make_async_remote_copy(
            src_ref=lag_send.at[peer // share],
            dst_ref=lags.at[me],
            send_sem=lag_sems.at[0, step],
            recv_sem=lag_sems.at[1, step],
            device_id={"seq": peer},
            device_id_type=MESH,
        )

    def remote(kind, source, target, chunk, step):
        peer = lax.rem(me + step, n)
        return pltpu.make_async_remote_copy(
            src_ref=source.at[chunk, peer],
            dst_ref=target.at[chunk, me],
            send_sem=sems.at[2 * kind, chunk, step],
            recv_sem=sems.at[2 * kind + 1, chunk, step],
            device_id={"seq": peer},
            device_id_type=MESH,
        )

    def value_copy(chunk, step):
        return remote(0, outgoing, held, chunk, step)

    def back_copy(chunk, step):
        return remote(1, result, returned, chunk, step)

    def send_block(off, chunk, make):
        inside = lax.rem(me, per)
        for turn in range(1 if off == blocks - 1 else 0, per):
            peer = place(off) * per + lax.rem(inside + turn, per)
            make(chunk, lax.rem(peer - me + n, n)).start()

    tokens_load.wait()
    for off in order:
        value_load(off).wait()
        block = jnp.dot(tokens[...], value_w[off], preferred_element_type=jnp.float32)
        block = block.astype(jnp.bfloat16).T.reshape(per, chunks, wide, rows)
        for chunk in range(chunks):
            outgoing[chunk, pl.ds(place(off) * per, per)] = block[:, chunk]
        if off == 0:
            pl.semaphore_wait(barrier, n - 1)
        send_block(off, 0, value_copy)
        if off == 0:
            gate_load.start()
            out_load.start()
            logits = lax.dot_general(
                head_ref[...], tokens[...], (((1,), (1,)), ((), ())), preferred_element_type=jnp.float32
            )
            for head in range(heads):
                made = jnp.tanh(logits[head : head + 1] + bias_ref[0, head]) * length ** (-0.5)
                lag_send[head] = made.astype(jnp.bfloat16).astype(jnp.float32)
            loop(lambda step: lag_copy(step).start())
            lags[me] = lag_send[me // share]
    for chunk in range(1, chunks):
        for off in order:
            send_block(off, chunk, value_copy)
    for chunk in range(chunks):
        held[chunk, me] = outgoing[chunk, me]

    loop(lambda step: lag_copy(step).wait())
    row = jnp.concatenate([lags[source] for source in range(n)], axis=1)
    row = jnp.concatenate([row[:, length - rows - LANES :], row], axis=1)
    for start in range(0, length + rows, rows):
        piece = jnp.broadcast_to(row[:, start : start + rows + LANES], (LANES, rows + LANES))
        turned = pltpu.roll(piece, 0, 1, stride=1, stride_axis=0)[:, LANES:]
        band[:, start : start + rows] = turned.astype(jnp.bfloat16)

    gate_load.wait()
    for part in range(model // BLOCK):
        gate = jnp.dot(
            tokens[...], gate_w[:, part * BLOCK : (part + 1) * BLOCK], preferred_element_type=jnp.float32
        )
        gate = (gate / (1.0 + jnp.exp(-gate))).T.reshape(per, chunks, wide, rows)
        for chunk in range(chunks):
            open_gate[chunk, part * per : (part + 1) * per] = gate[:, chunk]

    group = min(n, max(1, BLOCK // wide))
    reach = min(n, 16)

    def convolve(chunk, carry):
        loop(lambda step: value_copy(chunk, step).wait())
        held[chunk, n : 2 * n] = held[chunk, 0:n]

        def outputs(index, inner):
            first = index * group
            summed = None
            for base in range(0, n, reach):
                left = jnp.concatenate(
                    [
                        held[chunk, pl.ds(first + at, group)].reshape(group * wide, rows)
                        for at in range(base, base + reach)
                    ],
                    axis=1,
                )
                right = jnp.concatenate(
                    [
                        band[:, pl.ds((rows - at) if at <= rows else length + rows - at, rows)]
                        for at in range(base * rows, (base + reach) * rows, LANES)
                    ],
                    axis=0,
                )
                term = jnp.dot(left, right, preferred_element_type=jnp.float32)
                summed = term if summed is None else summed + term
            result[chunk, pl.ds(first, group)] = summed.astype(jnp.bfloat16).reshape(group, wide, rows)
            return inner

        lax.fori_loop(0, n // group, outputs, 0)
        for off in order:
            send_block(off, chunk, back_copy)
        returned[chunk, me] = result[chunk, me]
        return carry

    lax.fori_loop(0, chunks, convolve, 0)

    out_load.wait()
    part = n // 2
    for chunk in range(chunks):
        for far in range(2):
            base = (me // part) * part if far == 0 else (1 - me // part) * part

            def arrive(index, carry):
                step = lax.rem(me - (base + index) + n, n)

                @pl.when(step > 0)
                def _():
                    back_copy(chunk, step).wait_recv()

                return carry

            lax.fori_loop(0, part, arrive, 0)
            chosen = pl.ds(base, part)
            gated = returned[chunk, chosen].astype(jnp.float32) * open_gate[chunk, chosen]
            gated = gated.astype(jnp.bfloat16).reshape(part * wide, rows).T
            weight = out_w[chosen, chunk].reshape(part * wide, model)
            term = jnp.dot(gated, weight, preferred_element_type=jnp.float32)
            if chunk + far > 0:
                term = total[...] + term
            if chunk + far < chunks:
                total[...] = term
            else:
                mixed_ref[...] = term.astype(jnp.bfloat16)
    for chunk in range(chunks):
        loop(lambda step: back_copy(chunk, step).wait_send())


def body(tokens, value_weight, gate_weight, out_weight, kernel_weight, kernel_bias):
    rows, model = tokens.shape
    heads = kernel_weight.shape[1]
    n = lax.axis_size("seq")
    width = model // n
    chunks = max(1, min(CHUNKS, width // 16))
    wide = width // chunks
    length = rows * n
    per = BLOCK // width
    vmem = pl.BlockSpec(memory_space=pltpu.VMEM)
    anywhere = pl.BlockSpec(memory_space=pl.ANY)
    half = jnp.bfloat16
    return pl.pallas_call(
        functools.partial(layer_kernel, n, heads),
        out_shape=jax.ShapeDtypeStruct((rows, model), half),
        in_specs=[anywhere] * 4 + [vmem, pl.BlockSpec(memory_space=pltpu.SMEM)],
        out_specs=vmem,
        scratch_shapes=[
            pltpu.VMEM((rows, model), half),
            pltpu.VMEM((n // per, model, BLOCK), half),
            pltpu.VMEM((model, model), half),
            pltpu.VMEM((n, chunks, wide, model), half),
            pltpu.VMEM((chunks, n, wide, rows), half),
            pltpu.VMEM((chunks, 2 * n, wide, rows), half),
            pltpu.VMEM((heads, 1, rows), jnp.float32),
            pltpu.VMEM((n, 1, rows), jnp.float32),
            pltpu.VMEM((LANES, length + rows), half),
            pltpu.VMEM((chunks, n, wide, rows), jnp.float32),
            pltpu.VMEM((chunks, n, wide, rows), half),
            pltpu.VMEM((chunks, n, wide, rows), half),
            pltpu.VMEM((rows, model), jnp.float32),
            pltpu.SemaphoreType.DMA((3 + n // per,)),
            pltpu.SemaphoreType.DMA((2, n)),
            pltpu.SemaphoreType.DMA((4, chunks, n)),
        ],
        compiler_params=pltpu.CompilerParams(
            collective_id=0, has_side_effects=True, vmem_limit_bytes=60 * 2**20
        ),
    )(
        tokens,
        value_weight,
        gate_weight,
        out_weight.reshape(n, chunks, wide, model),
        kernel_weight.T,
        kernel_bias.reshape(1, heads),
    )


def solution(mesh):
    placed = (P(("grp", "seq"), None), P(), P(), P(), P(), P())
    return jax.shard_map(
        body, mesh=mesh, in_specs=placed, out_specs=P(("grp", "seq"), None), check_vma=False
    )
```
